32 devices in a mesh: req: 8 (over z, x), mlp: 4 (over y, core).
Axes of the slice: x: 2, y: 2, z: 4, core: 2. Of those that a mesh axis runs over, the one named last changes fastest.
Arguments:
- tokens: bfloat16 [8192, 2048], P('req'), may hold values from -6 to 6
- first_gain: float32 [2048], replicated, may hold values from 0.5 to 1.5
- joined_weight: bfloat16 [2048, 6144], P(None, 'mlp'), may hold values from -0.125 to 0.125
- dense_weight: bfloat16 [2048, 2048], P('mlp'), may hold values from -0.125 to 0.125
- adapter_down: bfloat16 [64, 16, 2048], P('req', None, 'mlp'), may hold values from -0.125 to 0.125
- adapter_up: bfloat16 [64, 16, 2048], P('req'), may hold values from -1.5 to 1.5
- adapter_ids: int32 [64], replicated, may hold values from 0 to 63, as said below
- adapter_rows: int32 [64], replicated, may hold values from 0 to 63, each once
- second_gain: float32 [2048], replicated, may hold values from 0.5 to 1.5
- up_weight: bfloat16 [2048, 8192], P(None, 'mlp'), may hold values from -0.125 to 0.125
- down_weight: bfloat16 [8192, 2048], P('mlp'), may hold values from -0.0625 to 0.0625
- page_pool: bfloat16 [96, 128, 4096], P('req', None, 'mlp'), may hold values from -100 to 100
- page_table: int32 [16, 4], P('req'), may hold values from 0 to 11, as said below
- group_index: int32 [64], P('req'), may hold values from 0 to 1
- lengths: int32 [64], P('req'), may hold values from 1 to 128, as said below
- migrants: int32 [32], P('req'), may hold values from 0 to 7, as said below
- landing: int32 [32], replicated, may hold values from 0 to 63, as said below
Outputs:
- layer_out: bfloat16 [8192, 2048], P(('req', 'mlp'))
- page_out: bfloat16 [64, 128, 4096], P('req', None, 'mlp')
The draws below stay inside these ranges and needn't reach their ends.
Inputs may be any that keep to these rules, and one draw needn't show every extreme that they name: `adapter_ids`: the requests name exactly 16 distinct adapters in all. `lengths`: each request owner holds at least one request of 128 tokens. `page_table`: the 8 entries of one owner's rows are distinct. `migrants`: entries m // 4 = o name 4 distinct requests of owner o. `landing`: A rearrangement of the slots (m // 4) * 8 + migrants[m] of all migrating requests; the 4 requests of one owner land on 4 distinct other owners, and every owner receives exactly 4 of them.
All inputs are finite; a program needn't handle non-finite values.
Results may differ from the reference program's by a relative error of at most 0.013.
The reference program's roundings to bfloat16 on the way count: a program that leaves them out, or rounds other values in their place, can miss the bound.
Values may be sent and summed in bfloat16 or wider, within the bound.
A program may use at most 192 MiB of HBM per device.

```python
import math
import jax
import jax.numpy as jnp
from jax import lax

D = 2048
HEADS = 16
HD = 128
FF = 8192
RANK = 16
ADAPTERS = 64
ACTIVE = 16
RQ_DEV = 8
SLOT = 128
PAGE = 128
PREF_PAGES = 4
GROUPS_DEV = 2
POOL_DEV = 12
MIG_DEV = 4
REQS = 64
TOKENS = 8192
N_REQ = 8
N_MLP = 4


def draw_page_pool(key, part):
    shape = (N_REQ * POOL_DEV, PAGE, 2 * D)
    first = jax.random.fold_in(key, 0)
    return jnp.clip(jax.random.normal(first, shape, jnp.float32), -6.0, 6.0).astype(jnp.bfloat16)


def draw_page_table(key, part):
    owner_keys = jax.random.split(key, N_REQ)
    orders = jax.vmap(lambda one: jax.random.permutation(one, POOL_DEV))(owner_keys)
    return orders[:, :GROUPS_DEV * PREF_PAGES].reshape(N_REQ * GROUPS_DEV, PREF_PAGES).astype(jnp.int32)


def draw_lengths(key, part):
    first, second, third = jax.random.split(key, 3)
    limit = jax.random.randint(first, (N_REQ, 1), SLOT // 4, SLOT + 1)
    lowest = jnp.maximum(limit // 2, 1)
    values = jax.random.randint(second, (N_REQ, RQ_DEV), lowest, limit + 1)
    longest = jax.random.randint(third, (N_REQ, 1), 0, RQ_DEV)
    values = jnp.where(jnp.arange(RQ_DEV)[None, :] == longest, SLOT, values)
    return values.reshape(-1).astype(jnp.int32)


def draw_adapter_ids(key, part):
    first, second, third = jax.random.split(key, 3)
    active_set = jax.random.permutation(first, ADAPTERS)[:ACTIVE]
    picked_rank = jax.random.randint(second, (REQS,), 0, ACTIVE)
    order = jax.random.permutation(third, REQS)
    picked_rank = picked_rank.at[order[:ACTIVE]].set(jnp.arange(ACTIVE))
    return active_set[picked_rank].astype(jnp.int32)


def migration_plan(key):
    base = jax.random.fold_in(key, 7)
    first, second, third, fourth = jax.random.split(base, 4)
    owner_keys = jax.random.split(first, N_REQ)
    orders = jax.vmap(lambda one: jax.random.permutation(one, RQ_DEV))(owner_keys)[:, :MIG_DEV]
    relabel = jax.random.permutation(second, N_REQ).astype(jnp.int32)
    inverse = jnp.argsort(relabel).astype(jnp.int32)
    shifts = (1 + jax.random.permutation(third, N_REQ - 1)[:MIG_DEV]).astype(jnp.int32)
    dest = inverse[(relabel[:, None] + shifts[None, :]) % N_REQ]
    slot_keys = jax.random.split(fourth, N_REQ)
    slot_orders = jax.vmap(lambda one: jax.random.permutation(one, MIG_DEV))(slot_keys).astype(jnp.int32)
    column = jnp.arange(MIG_DEV, dtype=jnp.int32)[None, :]
    picked = slot_orders[dest, jnp.broadcast_to(column, dest.shape)]
    targets = dest * RQ_DEV + orders[dest, picked]
    return (orders.reshape(-1), targets.reshape(-1))


def draw_migrants(key, part):
    return migration_plan(key)[0].astype(jnp.int32)


def draw_landing(key, part):
    return migration_plan(key)[1].astype(jnp.int32)


def with_ends(drawn, own_key, smallest, high):
    spot = [jax.random.randint(jax.random.fold_in(own_key, axis), (), 0, length) for axis, length in enumerate(drawn.shape)]
    main_axis = drawn.shape.index(max(drawn.shape))
    next_to = spot[:main_axis] + [(spot[main_axis] + 1) % drawn.shape[main_axis]] + spot[main_axis + 1:]
    return drawn.at[tuple(spot)].set(smallest).at[tuple(next_to)].set(high)


def levels(stream_key, dims, cuts, least, top_value):
    factor_of, own = 1.0, jax.random.fold_in(stream_key, 6)
    for position, parts in cuts:
        steps = jnp.exp(jax.random.uniform(jax.random.fold_in(own, position), (parts,), jnp.float32, least / len(cuts), top_value / len(cuts)))
        factor_of = factor_of * jnp.repeat(steps, dims[position] // parts).reshape([-1 if axis == position else 1 for axis in range(len(dims))])
    return factor_of


def bell_draw(stream_key, extent, spread, most, pieces=(), kind=jnp.bfloat16):
    array = spread * jax.random.normal(stream_key, extent, jnp.float32)
    if pieces:
        array = array * levels(stream_key, extent, pieces, -0.22, 0.18)
    return jnp.clip(array, -most, most).astype(kind)


def setup_inputs(seed: int = 0) -> dict:
    key_of = jax.random.split(jax.random.key(seed), 18)
    tokens = bell_draw(key_of[0], (TOKENS, D), 1.0, 6.0, ((0, 8),))
    first_gain = jnp.clip(1.0 + 0.1 * jax.random.normal(key_of[1], (D,), jnp.float32), 0.5, 1.5)
    joined_weight = bell_draw(key_of[2], (D, 3 * D), D ** -0.5, 0.125, ((1, 4),))
    dense_weight = bell_draw(key_of[3], (D, D), D ** -0.5, 0.125, ((0, 4),))
    adapter_down = bell_draw(key_of[4], (ADAPTERS, RANK, D), D ** -0.5, 0.125, ((0, 8), (2, 4)))
    adapter_up = bell_draw(key_of[5], (ADAPTERS, RANK, D), RANK ** -0.5, 1.5, ((0, 8),))
    adapter_ids = draw_adapter_ids(jax.random.fold_in(key_of[17], 71), 0)
    adapter_rows = jax.random.permutation(key_of[7], ADAPTERS).astype(jnp.int32)
    second_gain = jnp.clip(1.0 + 0.1 * jax.random.normal(key_of[8], (D,), jnp.float32), 0.5, 1.5)
    up_weight = bell_draw(key_of[9], (D, FF), D ** -0.5, 0.125, ((1, 4),))
    down_weight = bell_draw(key_of[10], (FF, D), FF ** -0.5, 0.0625, ((0, 4),))
    page_pool = draw_page_pool(jax.random.fold_in(key_of[17], 71), 0)
    page_table = draw_page_table(jax.random.fold_in(key_of[17], 71), 0)
    group_index = with_ends(jax.random.randint(key_of[13], (REQS,), 0, GROUPS_DEV), jax.random.fold_in(key_of[13], 1), 0, GROUPS_DEV - 1).astype(jnp.int32)
    lengths = draw_lengths(jax.random.fold_in(key_of[17], 71), 0)
    migrants = draw_migrants(jax.random.fold_in(key_of[17], 71), 0)
    landing = draw_landing(jax.random.fold_in(key_of[17], 71), 0)
    return {"tokens": tokens, "first_gain": first_gain, "joined_weight": joined_weight, "dense_weight": dense_weight, "adapter_down": adapter_down, "adapter_up": adapter_up, "adapter_ids": adapter_ids, "adapter_rows": adapter_rows, "second_gain": second_gain, "up_weight": up_weight, "down_weight": down_weight, "page_pool": page_pool, "page_table": page_table, "group_index": group_index, "lengths": lengths, "migrants": migrants, "landing": landing}


EPS = 1e-05

def layer_norm(values, gain):
    values = values.astype(jnp.float32)
    mean = lax.optimization_barrier(jnp.mean(values, axis=-1, keepdims=True))
    centred = values - mean
    variance = lax.optimization_barrier(jnp.mean(centred * centred, axis=-1, keepdims=True))
    return (centred * lax.rsqrt(variance + EPS) * gain.astype(jnp.float32)).astype(jnp.bfloat16)

def gelu_tanh(value):
    return 0.5 * value * (1.0 + jnp.tanh(0.7978845608 * (value + 0.044715 * value * value * value)))

def rounded(value):
    return lax.optimization_barrier(value.astype(jnp.bfloat16)).astype(jnp.float32)

def attend(queries, keys, values, prefix_keys, prefix_values, lens, slopes):
    scale = 1.0 / math.sqrt(queries.shape[-1])
    own_len = queries.shape[1]
    pre_len = prefix_keys.shape[1]
    query_f = queries.astype(jnp.float32)
    s_pre = jnp.einsum('rihe,rphe->rhip', query_f, prefix_keys.astype(jnp.float32)) * scale
    s_own = jnp.einsum('rihe,rjhe->rhij', query_f, keys.astype(jnp.float32)) * scale
    own_pos = jnp.arange(own_len).astype(jnp.float32)
    pre_pos = jnp.arange(pre_len).astype(jnp.float32)
    s_pre = s_pre - slopes[None, :, None, None] * ((pre_len + own_pos)[:, None] - pre_pos[None, :])[None, None]
    s_own = s_own - slopes[None, :, None, None] * (own_pos[:, None] - own_pos[None, :])[None, None]
    steps = jnp.arange(own_len, dtype=jnp.int32)
    allowed = (steps[None, :] <= steps[:, None])[None, None] & (steps[None, None, None, :] < lens[:, None, None, None])
    s_own = jnp.where(allowed, s_own, -jnp.inf)
    top = jnp.maximum(lax.optimization_barrier(jnp.max(s_pre, axis=-1)), lax.optimization_barrier(jnp.max(s_own, axis=-1)))[..., None]
    e_pre = jnp.exp(s_pre - top)
    e_own = jnp.exp(s_own - top)
    total = lax.optimization_barrier(jnp.sum(e_pre, axis=-1, keepdims=True)) + lax.optimization_barrier(jnp.sum(e_own, axis=-1, keepdims=True))
    w_pre = (e_pre / total).astype(jnp.bfloat16)
    w_own = (e_own / total).astype(jnp.bfloat16)
    mixed = jnp.einsum('rhip,rphe->rihe', w_pre.astype(jnp.float32), prefix_values.astype(jnp.float32))
    mixed = mixed + jnp.einsum('rhij,rjhe->rihe', w_own.astype(jnp.float32), values.astype(jnp.float32))
    return mixed.astype(jnp.bfloat16)

def reference(tokens, first_gain, joined_weight, dense_weight, adapter_down, adapter_up, adapter_ids, adapter_rows, second_gain, up_weight, down_weight, page_pool, page_table, group_index, lengths, migrants, landing):
    row_count = RQ_DEV * SLOT
    block = D // N_MLP
    hidden_block = FF // N_MLP
    head_pos = jnp.arange(HEADS).astype(jnp.float32)
    slopes = jnp.exp2(-8.0 * (head_pos + 1.0) / HEADS)
    table_rows = adapter_rows[adapter_ids]
    chosen_down = adapter_down[table_rows]
    chosen_up = adapter_up[table_rows]

    def one_owner(inputs):
        block_tokens, down_sel, up_sel, pool, table, groups, lens = inputs
        normed = layer_norm(block_tokens, first_gain)
        joined = jnp.dot(normed, joined_weight, preferred_element_type=jnp.float32).astype(jnp.bfloat16)
        joined = joined.reshape(RQ_DEV, SLOT, HEADS, 3, HD)
        valid = jnp.arange(SLOT, dtype=jnp.int32)[None, :] < lens[:, None]
        fresh = joined[:, :, :, 1:, :].reshape(RQ_DEV, SLOT, 2 * D)
        fresh = jnp.where(valid[:, :, None], fresh, jnp.zeros((), jnp.bfloat16))
        pages = table[groups]
        prefix = pool.reshape(POOL_DEV, PAGE, HEADS, 2, HD)[pages]
        prefix = prefix.reshape(RQ_DEV, PREF_PAGES * PAGE, HEADS, 2, HD)
        attended = attend(joined[:, :, :, 0], joined[:, :, :, 1], joined[:, :, :, 2], prefix[:, :, :, 0], prefix[:, :, :, 1], lens, slopes)
        attended_rows = attended.reshape(row_count, D)
        attended_req = attended.reshape(RQ_DEV, SLOT, D)
        dense = jnp.zeros((row_count, D), jnp.float32)
        low = jnp.zeros((RQ_DEV, SLOT, RANK), jnp.float32)
        for index in range(N_MLP):
            lo_col = index * block
            dense = dense + rounded(jnp.dot(attended_rows[:, lo_col:lo_col + block], dense_weight[lo_col:lo_col + block], preferred_element_type=jnp.float32))
            low = low + rounded(jnp.einsum('rsd,rkd->rsk', attended_req[:, :, lo_col:lo_col + block].astype(jnp.float32), down_sel[:, :, lo_col:lo_col + block].astype(jnp.float32)))
        low = low.astype(jnp.bfloat16)
        delta = jnp.einsum('rsk,rkd->rsd', low.astype(jnp.float32), up_sel.astype(jnp.float32)).reshape(row_count, D)
        residual = (block_tokens.astype(jnp.float32) + dense + delta).astype(jnp.bfloat16)
        normed_two = layer_norm(residual, second_gain)
        expanded = gelu_tanh(jnp.dot(normed_two, up_weight, preferred_element_type=jnp.float32)).astype(jnp.bfloat16)
        feed = jnp.zeros((row_count, D), jnp.float32)
        for index in range(N_MLP):
            lo_unit = index * hidden_block
            feed = feed + rounded(jnp.dot(expanded[:, lo_unit:lo_unit + hidden_block], down_weight[lo_unit:lo_unit + hidden_block], preferred_element_type=jnp.float32))
        result = jnp.where(valid.reshape(row_count)[:, None], residual.astype(jnp.float32) + feed, jnp.zeros((), jnp.float32))
        return (result.astype(jnp.bfloat16), fresh)
    outputs, fresh_all = lax.map(one_owner, (tokens.reshape(N_REQ, row_count, D), chosen_down.reshape(N_REQ, RQ_DEV, RANK, D), chosen_up.reshape(N_REQ, RQ_DEV, RANK, D), page_pool.reshape(N_REQ, POOL_DEV, PAGE, 2 * D), page_table.reshape(N_REQ, GROUPS_DEV, PREF_PAGES), group_index.reshape(N_REQ, RQ_DEV), lengths.reshape(N_REQ, RQ_DEV)))
    layer_out = outputs.reshape(TOKENS, D)
    fresh_all = fresh_all.reshape(REQS, SLOT, 2 * D)
    sources = jnp.arange(N_REQ * MIG_DEV, dtype=jnp.int32) // MIG_DEV * RQ_DEV + migrants.astype(jnp.int32)
    anchor = jnp.arange(REQS, dtype=jnp.int32).at[landing.astype(jnp.int32)].set(sources)
    page_out = fresh_all[anchor]
    return (layer_out, page_out)
```

```python
import functools
import math

import jax
import jax.numpy as jnp
from jax import lax
from jax.experimental import pallas as pl
from jax.experimental.pallas import tpu as pltpu
from jax.sharding import PartitionSpec as P

HEADS = 16
HD = 128
ADAPTERS = 64
CORES = 2


EPS = 1e-05


def layer_norm(values, gain):
    values = values.astype(jnp.float32)
    mean = jnp.mean(values, axis=-1, keepdims=True)
    centred = values - mean
    variance = jnp.mean(centred * centred, axis=-1, keepdims=True)
    return (centred * lax.rsqrt(variance + EPS) * gain).astype(jnp.bfloat16)


def gelu_tanh(value):
    return 0.5 * value * (1.0 + jnp.tanh(0.7978845608 * (value + 0.044715 * value * value * value)))


def attend_body(local_heads, n_pages, order, pages, lens, slopes, joined, *refs):
    page_refs = refs[:n_pages]
    dense_w = refs[n_pages]
    attended, fresh, dense = refs[n_pages + 1 :]
    request = order[pl.program_id(0)]
    length = lens[request]
    slot = joined.shape[0]
    pre_len = n_pages * page_refs[0].shape[1]
    total_len = pre_len + slot
    scale = 1.0 / math.sqrt(HD)
    row = lax.broadcasted_iota(jnp.int32, (slot, total_len), 0)
    col = lax.broadcasted_iota(jnp.int32, (slot, total_len), 1)
    distance = (pre_len + row - col).astype(jnp.float32)
    allowed = (col < pre_len) | ((col - pre_len <= row) & (col - pre_len < length))
    valid = lax.broadcasted_iota(jnp.int32, (slot, 2 * HD), 0) < length
    for h in range(local_heads):
        base = h * 3 * HD
        query = joined[:, base : base + HD]
        own = joined[:, base + HD : base + 3 * HD]
        fresh[0, :, h * 2 * HD : (h + 1) * 2 * HD] = jnp.where(
            valid, own, jnp.zeros((), jnp.bfloat16)
        )
        keys = jnp.concatenate(
            [p[0, :, h * 2 * HD : h * 2 * HD + HD] for p in page_refs] + [own[:, :HD]], axis=0
        )
        values = jnp.concatenate(
            [p[0, :, h * 2 * HD + HD : (h + 1) * 2 * HD] for p in page_refs] + [own[:, HD:]],
            axis=0,
        )
        scores = lax.dot_general(
            query, keys, (((1,), (1,)), ((), ())), preferred_element_type=jnp.float32
        )
        scores = jnp.where(allowed, scores * scale - slopes[h] * distance, -jnp.inf)
        top = jnp.max(scores, axis=-1, keepdims=True)
        weights = jnp.exp(scores - top)
        total = jnp.sum(weights, axis=-1, keepdims=True)
        weights = (weights / total).astype(jnp.bfloat16)
        mixed = jnp.dot(weights, values, preferred_element_type=jnp.float32)
        attended[:, h * HD : (h + 1) * HD] = mixed.astype(jnp.bfloat16)
    dense[...] = jnp.dot(
        attended[...], dense_w[...], preferred_element_type=jnp.float32
    ).astype(jnp.bfloat16)


def attend(joined, pool, pages, lens, slopes, order, dense_weight, slot):
    count = order.shape[0]
    n_pages = pages.shape[1]
    width = joined.shape[1]
    local_heads = width // (3 * HD)
    page_specs = [
        pl.BlockSpec(
            (1, pool.shape[1], pool.shape[2]),
            functools.partial(lambda p, i, o, pg, ln, sl: (pg[o[i], p], 0, 0), p),
        )
        for p in range(n_pages)
    ]
    return pl.pallas_call(
        functools.partial(attend_body, local_heads, n_pages),
        grid_spec=pltpu.PrefetchScalarGridSpec(
            num_scalar_prefetch=4,
            grid=(count,),
            in_specs=[pl.BlockSpec((slot, width), lambda i, o, pg, ln, sl: (o[i], 0))]
            + page_specs
            + [pl.BlockSpec(dense_weight.shape, lambda i, o, pg, ln, sl: (0, 0))],
            out_specs=[
                pl.BlockSpec((slot, local_heads * HD), lambda i, o, pg, ln, sl: (i, 0)),
                pl.BlockSpec((1, slot, local_heads * 2 * HD), lambda i, o, pg, ln, sl: (i, 0, 0)),
                pl.BlockSpec((slot, dense_weight.shape[1]), lambda i, o, pg, ln, sl: (i, 0)),
            ],
        ),
        out_shape=[
            jax.ShapeDtypeStruct((count * slot, local_heads * HD), jnp.bfloat16),
            jax.ShapeDtypeStruct((count, slot, local_heads * 2 * HD), jnp.bfloat16),
            jax.ShapeDtypeStruct((count * slot, dense_weight.shape[1]), jnp.bfloat16),
        ],
        compiler_params=pltpu.CompilerParams(vmem_limit_bytes=40 * 1024 * 1024),
        cost_estimate=pl.CostEstimate(
            flops=6 * 10**9 * count // 8, bytes_accessed=2 * 10**7 * count // 8, transcendentals=0
        ),
    )(order, pages, lens, slopes, joined, *([pool] * n_pages), dense_weight)


def merge_body(source, came, fresh, arrived, out):
    here = came[pl.program_id(0)]

    @pl.when(here == 0)
    def _():
        out[...] = fresh[...]

    @pl.when(here != 0)
    def _():
        out[...] = arrived[...]


def merge(fresh, place, arrived, source, came):
    requests = came.shape[0]
    block = (1,) + fresh.shape[1:]
    return pl.pallas_call(
        lambda place, source, came, *refs: merge_body(source, came, *refs),
        grid_spec=pltpu.PrefetchScalarGridSpec(
            num_scalar_prefetch=3,
            grid=(requests,),
            in_specs=[
                pl.BlockSpec(block, lambda i, p, s, c: (p[i], 0, 0)),
                pl.BlockSpec(block, lambda i, p, s, c: (s[i], 0, 0)),
            ],
            out_specs=pl.BlockSpec(block, lambda i, p, s, c: (i, 0, 0)),
        ),
        out_shape=jax.ShapeDtypeStruct(fresh.shape, fresh.dtype),
    )(place, source, came, fresh, arrived)


def shards(
    tokens,
    first_gain,
    joined_weight,
    dense_weight,
    adapter_down,
    adapter_up,
    adapter_ids,
    adapter_rows,
    second_gain,
    up_weight,
    down_weight,
    page_pool,
    page_table,
    group_index,
    lengths,
    migrants,
    landing,
):
    mlp_count = lax.axis_size("mlp")
    req_count = lax.axis_size("req")
    req_index = lax.axis_index("req")
    mlp_index = lax.axis_index("mlp")
    requests = lengths.shape[0]
    slot = tokens.shape[0] // requests
    width = tokens.shape[1]
    local_heads = joined_weight.shape[1] // (3 * HD)
    own_requests = requests // mlp_count
    rows = mlp_count // CORES
    row_index = mlp_index // CORES
    core_index = mlp_index % CORES
    core_pairs = [(m, m ^ 1) for m in range(mlp_count)]

    def across_rows(values):
        out = [values]
        for k in range(1, rows):
            pairs = [(m, (m + k * CORES) % mlp_count) for m in range(mlp_count)]
            out.append(lax.ppermute(values, "mlp", pairs))
        return out

    local_ids = lax.dynamic_slice_in_dim(adapter_ids, req_index * requests, requests)
    table_rows = adapter_rows[local_ids]
    cols = adapter_down.shape[2]
    own_up = lax.dynamic_slice_in_dim(adapter_up, mlp_index * cols, cols, axis=2)
    tables = lax.all_gather(
        jnp.concatenate([adapter_down, own_up], axis=2), "req", axis=0, tiled=True
    )
    chosen = tables[table_rows]
    chosen_down = chosen[:, :, :cols]
    chosen_up = lax.all_gather(chosen[:, :, cols:], "mlp", axis=2, tiled=True)

    normed = layer_norm(tokens, first_gain)
    joined = jnp.dot(normed, joined_weight, preferred_element_type=jnp.float32).astype(jnp.bfloat16)
    pages = page_table[group_index]
    head_pos = (mlp_index * local_heads + jnp.arange(local_heads, dtype=jnp.int32)).astype(
        jnp.float32
    )
    slopes = jnp.exp2(-8.0 * (head_pos + 1.0) / HEADS)

    grid_rows = jnp.arange(rows, dtype=jnp.int32)[None, :]
    grid_cores = (jnp.arange(CORES, dtype=jnp.int32)[:, None] + core_index) % CORES
    orders = [
        ((grid_rows * CORES + grid_cores) * own_requests + c).reshape(-1)
        for c in range(own_requests)
    ]
    half = rows * slot
    firsts = []
    freshes = []
    for c in range(own_requests):
        attended, fresh_c, dense_part = attend(
            joined, page_pool, pages, lengths, slopes, orders[c], dense_weight, slot
        )
        freshes.append(fresh_c)
        firsts.append((attended, dense_part))
    fresh = jnp.concatenate(freshes, axis=0)
    order = jnp.concatenate(orders)
    place = jnp.argmax(
        (order[None, :] == jnp.arange(requests, dtype=jnp.int32)[:, None]).astype(jnp.int32), axis=1
    ).astype(jnp.int32)

    outs = []
    for c in range(own_requests):
        attended, dense_part = firsts[c]
        low_part = lax.dot_general(
            chosen_down[orders[c]],
            attended.reshape(mlp_count, slot, local_heads * HD),
            (((2,), (2,)), ((0,), (0,))),
            preferred_element_type=jnp.float32,
        ).astype(jnp.bfloat16)
        in_order = jnp.arange(mlp_count, dtype=jnp.int32) // CORES
        swap = in_order + (
            (jnp.arange(mlp_count, dtype=jnp.int32) % CORES + core_index) % CORES
        ) * rows
        every_low = lax.all_gather(low_part[swap], "mlp", axis=0, tiled=False)
        low_all = jnp.sum(every_low.astype(jnp.float32), axis=0).astype(jnp.bfloat16)
        mine = orders[c][:rows]
        low = low_all.reshape(rows, CORES, low_all.shape[1], slot)
        low = lax.dynamic_index_in_dim(low, core_index, axis=1, keepdims=False)
        delta = lax.dot_general(
            low,
            chosen_up[mine],
            (((1,), (1,)), ((0,), (0,))),
            preferred_element_type=jnp.float32,
        ).reshape(half, width)
        other = lax.ppermute(dense_part[half:], "mlp", core_pairs)
        pair_sum = (dense_part[:half].astype(jnp.float32) + other.astype(jnp.float32)).astype(
            jnp.bfloat16
        )
        dense = sum(part.astype(jnp.float32) for part in across_rows(pair_sum))
        own_tokens = tokens.reshape(rows, CORES, own_requests, slot, width)[:, :, c]
        own_tokens = lax.dynamic_index_in_dim(own_tokens, core_index, axis=1, keepdims=False)
        residual = (
            own_tokens.reshape(half, width).astype(jnp.float32) + dense + delta
        ).astype(jnp.bfloat16)
        normed_two = layer_norm(residual, second_gain)
        theirs = lax.ppermute(normed_two, "mlp", core_pairs)
        expanded = gelu_tanh(
            jnp.dot(
                jnp.concatenate([normed_two, theirs], axis=0),
                up_weight,
                preferred_element_type=jnp.float32,
            )
        ).astype(jnp.bfloat16)
        part = jnp.dot(expanded, down_weight, preferred_element_type=jnp.float32).astype(
            jnp.bfloat16
        )
        other = lax.ppermute(part[half:], "mlp", core_pairs)
        pair_sum = (part[:half].astype(jnp.float32) + other.astype(jnp.float32)).astype(
            jnp.bfloat16
        ).reshape(rows, slot, width)
        feed = lax.dynamic_index_in_dim(pair_sum, row_index, axis=0, keepdims=False).astype(
            jnp.float32
        )
        for k in range(1, rows):
            pairs = [(m, (m + k * CORES) % mlp_count) for m in range(mlp_count)]
            send = lax.dynamic_index_in_dim(
                pair_sum, (row_index + k) % rows, axis=0, keepdims=False
            )
            feed = feed + lax.ppermute(send, "mlp", pairs).astype(jnp.float32)
        own_res = lax.dynamic_index_in_dim(
            residual.reshape(rows, slot, width), row_index, axis=0, keepdims=False
        )
        length = lengths[mlp_index * own_requests + c]
        own_valid = jnp.arange(slot, dtype=jnp.int32) < length
        outs.append(
            jnp.where(
                own_valid[:, None], own_res.astype(jnp.float32) + feed, jnp.zeros((), jnp.float32)
            ).astype(jnp.bfloat16)
        )
    layer_out = jnp.concatenate(outs, axis=0)

    moves = migrants.shape[0]
    my_landing = lax.dynamic_slice_in_dim(landing, req_index * moves, moves)
    own_slots = req_index * requests + jnp.arange(requests, dtype=jnp.int32)
    lands_here = landing[None, :] == own_slots[:, None]
    came = jnp.any(lands_here, axis=1).astype(jnp.int32)
    owner = jnp.argmax(lands_here.astype(jnp.int32), axis=1).astype(jnp.int32) // moves
    arrived = []
    for k in range(1, req_count):
        to = (req_index + k) % req_count
        hit = (my_landing // requests == to).astype(jnp.int32)
        send = lax.dynamic_index_in_dim(
            fresh, place[jnp.sum(hit * migrants)], axis=0, keepdims=True
        )
        pairs = [(r, (r + k) % req_count) for r in range(req_count)]
        arrived.append(lax.ppermute(send, "req", pairs))
    arrived = jnp.concatenate(arrived, axis=0)
    source = jnp.where(came > 0, (req_index - owner - 1) % req_count, 0).astype(jnp.int32)
    source = jnp.clip(source, 0, req_count - 2)
    page_out = merge(fresh, place, arrived, source, came)
    return (layer_out, page_out)


def solution(mesh):
    return jax.shard_map(
        shards,
        mesh=mesh,
        in_specs=(
            P("req", None),
            P(),
            P(None, "mlp"),
            P("mlp", None),
            P("req", None, "mlp"),
            P("req", None, None),
            P(),
            P(),
            P(),
            P(None, "mlp"),
            P("mlp", None),
            P("req", None, "mlp"),
            P("req", None),
            P("req"),
            P("req"),
            P("req"),
            P(),
        ),
        out_specs=(P(("req", "mlp"), None), P("req", None, "mlp")),
        check_vma=False,
    )
```

```python
import functools
import math

import jax
import jax.numpy as jnp
from jax import lax
from jax.experimental import pallas as pl
from jax.experimental.pallas import tpu as pltpu
from jax.sharding import PartitionSpec as P

HEADS = 16
HD = 128
ADAPTERS = 64
ACTIVE = 16
CORES = 2


EPS = 1e-05


def layer_norm(values, gain):
    values = values.astype(jnp.float32)
    mean = jnp.mean(values, axis=-1, keepdims=True)
    centred = values - mean
    variance = jnp.mean(centred * centred, axis=-1, keepdims=True)
    return (centred * lax.rsqrt(variance + EPS) * gain).astype(jnp.bfloat16)


def gelu_tanh(value):
    return 0.5 * value * (1.0 + jnp.tanh(0.7978845608 * (value + 0.044715 * value * value * value)))


def attend_body(local_heads, n_pages, order, pages, lens, slopes, joined, *refs):
    page_refs = refs[:n_pages]
    dense_w = refs[n_pages]
    attended, fresh, dense = refs[n_pages + 1 :]
    request = order[pl.program_id(0)]
    length = lens[request]
    slot = joined.shape[0]
    pre_len = n_pages * page_refs[0].shape[1]
    total_len = pre_len + slot
    scale = 1.0 / math.sqrt(HD)
    row = lax.broadcasted_iota(jnp.int32, (slot, total_len), 0)
    col = lax.broadcasted_iota(jnp.int32, (slot, total_len), 1)
    distance = (pre_len + row - col).astype(jnp.float32)
    allowed = (col < pre_len) | ((col - pre_len <= row) & (col - pre_len < length))
    valid = lax.broadcasted_iota(jnp.int32, (slot, 2 * HD), 0) < length
    for h in range(local_heads):
        base = h * 3 * HD
        query = joined[:, base : base + HD]
        own = joined[:, base + HD : base + 3 * HD]
        fresh[0, :, h * 2 * HD : (h + 1) * 2 * HD] = jnp.where(
            valid, own, jnp.zeros((), jnp.bfloat16)
        )
        keys = jnp.concatenate(
            [p[0, :, h * 2 * HD : h * 2 * HD + HD] for p in page_refs] + [own[:, :HD]], axis=0
        )
        values = jnp.concatenate(
            [p[0, :, h * 2 * HD + HD : (h + 1) * 2 * HD] for p in page_refs] + [own[:, HD:]],
            axis=0,
        )
        scores = lax.dot_general(
            query, keys, (((1,), (1,)), ((), ())), preferred_element_type=jnp.float32
        )
        scores = jnp.where(allowed, scores * scale - slopes[h] * distance, -jnp.inf)
        top = jnp.max(scores, axis=-1, keepdims=True)
        weights = jnp.exp(scores - top)
        total = jnp.sum(weights, axis=-1, keepdims=True)
        weights = (weights / total).astype(jnp.bfloat16)
        mixed = jnp.dot(weights, values, preferred_element_type=jnp.float32)
        attended[:, h * HD : (h + 1) * HD] = mixed.astype(jnp.bfloat16)
    dense[...] = jnp.dot(
        attended[...], dense_w[...], preferred_element_type=jnp.float32
    ).astype(jnp.bfloat16)


def attend(joined, pool, pages, lens, slopes, order, dense_weight, slot):
    count = order.shape[0]
    n_pages = pages.shape[1]
    width = joined.shape[1]
    local_heads = width // (3 * HD)
    page_specs = [
        pl.BlockSpec(
            (1, pool.shape[1], pool.shape[2]),
            functools.partial(lambda p, i, o, pg, ln, sl: (pg[o[i], p], 0, 0), p),
        )
        for p in range(n_pages)
    ]
    return pl.pallas_call(
        functools.partial(attend_body, local_heads, n_pages),
        grid_spec=pltpu.PrefetchScalarGridSpec(
            num_scalar_prefetch=4,
            grid=(count,),
            in_specs=[pl.BlockSpec((slot, width), lambda i, o, pg, ln, sl: (o[i], 0))]
            + page_specs
            + [pl.BlockSpec(dense_weight.shape, lambda i, o, pg, ln, sl: (0, 0))],
            out_specs=[
                pl.BlockSpec((slot, local_heads * HD), lambda i, o, pg, ln, sl: (i, 0)),
                pl.BlockSpec((1, slot, local_heads * 2 * HD), lambda i, o, pg, ln, sl: (i, 0, 0)),
                pl.BlockSpec((slot, dense_weight.shape[1]), lambda i, o, pg, ln, sl: (i, 0)),
            ],
        ),
        out_shape=[
            jax.ShapeDtypeStruct((count * slot, local_heads * HD), jnp.bfloat16),
            jax.ShapeDtypeStruct((count, slot, local_heads * 2 * HD), jnp.bfloat16),
            jax.ShapeDtypeStruct((count * slot, dense_weight.shape[1]), jnp.bfloat16),
        ],
        compiler_params=pltpu.CompilerParams(vmem_limit_bytes=40 * 1024 * 1024),
        cost_estimate=pl.CostEstimate(
            flops=6 * 10**9 * count // 8, bytes_accessed=2 * 10**7 * count // 8, transcendentals=0
        ),
    )(order, pages, lens, slopes, joined, *([pool] * n_pages), dense_weight)


def merge_body(distance, fresh, *refs):
    here = distance[pl.program_id(0)]
    out = refs[-1]

    @pl.when(here == 0)
    def _():
        out[...] = fresh[...]

    for k in range(1, len(refs)):

        @pl.when(here == k)
        def _(k=k):
            out[...] = refs[k - 1][...]


def merge(fresh, place, arrived, distance):
    requests = distance.shape[0]
    block = (1,) + fresh.shape[1:]
    return pl.pallas_call(
        lambda place, distance, *refs: merge_body(distance, *refs),
        grid_spec=pltpu.PrefetchScalarGridSpec(
            num_scalar_prefetch=2,
            grid=(requests,),
            in_specs=[pl.BlockSpec(block, lambda i, p, d: (p[i], 0, 0))]
            + [pl.BlockSpec(block, lambda i, p, d: (0, 0, 0))] * len(arrived),
            out_specs=pl.BlockSpec(block, lambda i, p, d: (i, 0, 0)),
        ),
        out_shape=jax.ShapeDtypeStruct(fresh.shape, fresh.dtype),
        compiler_params=pltpu.CompilerParams(vmem_limit_bytes=20 * 1024 * 1024),
    )(place, distance, fresh, *arrived)


def shards(
    tokens,
    first_gain,
    joined_weight,
    dense_weight,
    adapter_down,
    adapter_up,
    adapter_ids,
    adapter_rows,
    second_gain,
    up_weight,
    down_weight,
    page_pool,
    page_table,
    group_index,
    lengths,
    migrants,
    landing,
):
    mlp_count = lax.axis_size("mlp")
    req_count = lax.axis_size("req")
    req_index = lax.axis_index("req")
    mlp_index = lax.axis_index("mlp")
    requests = lengths.shape[0]
    slot = tokens.shape[0] // requests
    width = tokens.shape[1]
    local_heads = joined_weight.shape[1] // (3 * HD)
    own_requests = requests // mlp_count
    rows = mlp_count // CORES
    row_index = mlp_index // CORES
    core_index = mlp_index % CORES
    core_pairs = [(m, m ^ 1) for m in range(mlp_count)]

    def across_rows(values):
        out = [values]
        for k in range(1, rows):
            pairs = [(m, (m + k * CORES) % mlp_count) for m in range(mlp_count)]
            out.append(lax.ppermute(values, "mlp", pairs))
        return out

    local_ids = lax.dynamic_slice_in_dim(adapter_ids, req_index * requests, requests)
    table_rows = adapter_rows[local_ids]
    cols = adapter_down.shape[2]
    own_up = lax.dynamic_slice_in_dim(adapter_up, mlp_index * cols, cols, axis=2)
    used = jnp.any(
        adapter_rows[adapter_ids][:, None] == jnp.arange(ADAPTERS, dtype=jnp.int32)[None, :], axis=0
    )
    rank = jnp.cumsum(used.astype(jnp.int32)) - 1
    held = adapter_down.shape[0]
    held_rank = jnp.where(
        lax.dynamic_slice_in_dim(used, req_index * held, held),
        lax.dynamic_slice_in_dim(rank, req_index * held, held),
        -1,
    )
    put = jnp.arange(ACTIVE, dtype=jnp.int32)[:, None] == held_rank[None, :]
    spread = jnp.einsum(
        "ah,hkd->akd",
        put.astype(jnp.bfloat16),
        jnp.concatenate([adapter_down, own_up], axis=2),
        preferred_element_type=jnp.float32,
    ).astype(jnp.bfloat16)
    tables = lax.psum(spread, "req")
    chosen = tables[rank[table_rows]]
    chosen_down = chosen[:, :, :cols]
    up_parts = [chosen[:, :, cols:]]
    for k in range(1, mlp_count):
        pairs = [(m, (m + k) % mlp_count) for m in range(mlp_count)]
        up_parts.append(lax.ppermute(up_parts[0], "mlp", pairs))
    up_parts = jnp.stack(up_parts, axis=0)
    up_parts = up_parts[(mlp_index - jnp.arange(mlp_count, dtype=jnp.int32)) % mlp_count]

    normed = layer_norm(tokens, first_gain)
    joined = jnp.dot(normed, joined_weight, preferred_element_type=jnp.float32).astype(jnp.bfloat16)
    pages = page_table[group_index]
    head_pos = (mlp_index * local_heads + jnp.arange(local_heads, dtype=jnp.int32)).astype(
        jnp.float32
    )
    slopes = jnp.exp2(-8.0 * (head_pos + 1.0) / HEADS)

    grid_rows = jnp.arange(rows, dtype=jnp.int32)[None, :]
    grid_cores = (jnp.arange(CORES, dtype=jnp.int32)[:, None] + core_index) % CORES
    orders = [
        ((grid_rows * CORES + grid_cores) * own_requests + c).reshape(-1)
        for c in range(own_requests)
    ]
    half = rows * slot
    firsts = []
    freshes = []
    for c in range(own_requests):
        attended, fresh_c, dense_part = attend(
            joined, page_pool, pages, lengths, slopes, orders[c], dense_weight, slot
        )
        freshes.append(fresh_c)
        firsts.append((attended, dense_part))
    fresh = jnp.concatenate(freshes, axis=0)
    order = jnp.concatenate(orders)
    place = jnp.argmax(
        (order[None, :] == jnp.arange(requests, dtype=jnp.int32)[:, None]).astype(jnp.int32), axis=1
    ).astype(jnp.int32)

    every = jnp.concatenate([f[0].reshape(mlp_count, slot, local_heads * HD) for f in firsts])
    low_part = lax.dot_general(
        chosen_down[order], every, (((2,), (2,)), ((0,), (0,))), preferred_element_type=jnp.float32
    ).astype(jnp.bfloat16)[place]
    low_all = low_part.astype(jnp.float32)
    for k in range(1, mlp_count):
        pairs = [(m, (m + k) % mlp_count) for m in range(mlp_count)]
        low_all = low_all + lax.ppermute(low_part, "mlp", pairs).astype(jnp.float32)
    low_all = low_all.astype(jnp.bfloat16)

    outs = []
    for c in range(own_requests):
        attended, dense_part = firsts[c]
        mine = orders[c][:rows]
        low = low_all.reshape(rows, CORES, own_requests, low_all.shape[1], slot)[:, :, c]
        low = lax.dynamic_index_in_dim(low, core_index, axis=1, keepdims=False)
        own_ups = up_parts[:, mine]
        delta = jnp.concatenate(
            [
                lax.dot_general(
                    low,
                    own_ups[m],
                    (((1,), (1,)), ((0,), (0,))),
                    preferred_element_type=jnp.float32,
                )
                for m in range(mlp_count)
            ],
            axis=2,
        ).reshape(half, width)
        other = lax.ppermute(dense_part[half:], "mlp", core_pairs)
        pair_sum = (dense_part[:half].astype(jnp.float32) + other.astype(jnp.float32)).astype(
            jnp.bfloat16
        )
        dense = sum(part.astype(jnp.float32) for part in across_rows(pair_sum))
        own_tokens = tokens.reshape(rows, CORES, own_requests, slot, width)[:, :, c]
        own_tokens = lax.dynamic_index_in_dim(own_tokens, core_index, axis=1, keepdims=False)
        residual = (
            own_tokens.reshape(half, width).astype(jnp.float32) + dense + delta
        ).astype(jnp.bfloat16)
        normed_two = layer_norm(residual, second_gain)
        theirs = lax.ppermute(normed_two, "mlp", core_pairs)
        expanded = gelu_tanh(
            jnp.dot(
                jnp.concatenate([normed_two, theirs], axis=0),
                up_weight,
                preferred_element_type=jnp.float32,
            )
        ).astype(jnp.bfloat16)
        part = jnp.dot(expanded, down_weight, preferred_element_type=jnp.float32).astype(
            jnp.bfloat16
        )
        other = lax.ppermute(part[half:], "mlp", core_pairs)
        pair_sum = (part[:half].astype(jnp.float32) + other.astype(jnp.float32)).astype(
            jnp.bfloat16
        ).reshape(rows, slot, width)
        feed = lax.dynamic_index_in_dim(pair_sum, row_index, axis=0, keepdims=False).astype(
            jnp.float32
        )
        for k in range(1, rows):
            pairs = [(m, (m + k * CORES) % mlp_count) for m in range(mlp_count)]
            send = lax.dynamic_index_in_dim(
                pair_sum, (row_index + k) % rows, axis=0, keepdims=False
            )
            feed = feed + lax.ppermute(send, "mlp", pairs).astype(jnp.float32)
        own_res = lax.dynamic_index_in_dim(
            residual.reshape(rows, slot, width), row_index, axis=0, keepdims=False
        )
        length = lengths[mlp_index * own_requests + c]
        own_valid = jnp.arange(slot, dtype=jnp.int32) < length
        outs.append(
            jnp.where(
                own_valid[:, None], own_res.astype(jnp.float32) + feed, jnp.zeros((), jnp.float32)
            ).astype(jnp.bfloat16)
        )
    layer_out = jnp.concatenate(outs, axis=0)

    moves = migrants.shape[0]
    my_landing = lax.dynamic_slice_in_dim(landing, req_index * moves, moves)
    own_slots = req_index * requests + jnp.arange(requests, dtype=jnp.int32)
    lands_here = landing[None, :] == own_slots[:, None]
    came = jnp.any(lands_here, axis=1).astype(jnp.int32)
    owner = jnp.argmax(lands_here.astype(jnp.int32), axis=1).astype(jnp.int32) // moves
    arrived = []
    for k in range(1, req_count):
        to = (req_index + k) % req_count
        hit = (my_landing // requests == to).astype(jnp.int32)
        send = lax.dynamic_index_in_dim(
            fresh, place[jnp.sum(hit * migrants)], axis=0, keepdims=True
        )
        pairs = [(r, (r + k) % req_count) for r in range(req_count)]
        arrived.append(lax.ppermute(send, "req", pairs))
    distance = jnp.where(came > 0, (req_index - owner) % req_count, 0).astype(jnp.int32)
    page_out = merge(fresh, place, arrived, distance)
    return (layer_out, page_out)


def solution(mesh):
    return jax.shard_map(
        shards,
        mesh=mesh,
        in_specs=(
            P("req", None),
            P(),
            P(None, "mlp"),
            P("mlp", None),
            P("req", None, "mlp"),
            P("req", None, None),
            P(),
            P(),
            P(),
            P(None, "mlp"),
            P("mlp", None),
            P("req", None, "mlp"),
            P("req", None),
            P("req"),
            P("req"),
            P("req"),
            P(),
        ),
        out_specs=(P(("req", "mlp"), None), P("req", None, "mlp")),
        check_vma=False,
    )
```

```python
import functools
import math

import jax
import jax.numpy as jnp
from jax import lax
from jax.experimental import pallas as pl
from jax.experimental.pallas import tpu as pltpu
from jax.sharding import PartitionSpec as P

HEADS = 16
HD = 128
ADAPTERS = 64
CORES = 2


EPS = 1e-05


def layer_norm(values, gain):
    values = values.astype(jnp.float32)
    mean = jnp.mean(values, axis=-1, keepdims=True)
    centred = values - mean
    variance = jnp.mean(centred * centred, axis=-1, keepdims=True)
    return (centred * lax.rsqrt(variance + EPS) * gain).astype(jnp.bfloat16)


def gelu_tanh(value):
    return 0.5 * value * (1.0 + jnp.tanh(0.7978845608 * (value + 0.044715 * value * value * value)))


def attend_body(local_heads, n_pages, order, pages, lens, slopes, joined, *refs):
    page_refs = refs[:n_pages]
    dense_w = refs[n_pages]
    attended, fresh, dense = refs[n_pages + 1 :]
    request = order[pl.program_id(0)]
    length = lens[request]
    slot = joined.shape[0]
    pre_len = n_pages * page_refs[0].shape[1]
    total_len = pre_len + slot
    scale = 1.0 / math.sqrt(HD)
    row = lax.broadcasted_iota(jnp.int32, (slot, total_len), 0)
    col = lax.broadcasted_iota(jnp.int32, (slot, total_len), 1)
    distance = (pre_len + row - col).astype(jnp.float32)
    allowed = (col < pre_len) | ((col - pre_len <= row) & (col - pre_len < length))
    valid = lax.broadcasted_iota(jnp.int32, (slot, 2 * HD), 0) < length
    for h in range(local_heads):
        base = h * 3 * HD
        query = joined[:, base : base + HD]
        own = joined[:, base + HD : base + 3 * HD]
        fresh[0, :, h * 2 * HD : (h + 1) * 2 * HD] = jnp.where(
            valid, own, jnp.zeros((), jnp.bfloat16)
        )
        keys = jnp.concatenate(
            [p[0, :, h * 2 * HD : h * 2 * HD + HD] for p in page_refs] + [own[:, :HD]], axis=0
        )
        values = jnp.concatenate(
            [p[0, :, h * 2 * HD + HD : (h + 1) * 2 * HD] for p in page_refs] + [own[:, HD:]],
            axis=0,
        )
        scores = lax.dot_general(
            query, keys, (((1,), (1,)), ((), ())), preferred_element_type=jnp.float32
        )
        scores = jnp.where(allowed, scores * scale - slopes[h] * distance, -jnp.inf)
        top = jnp.max(scores, axis=-1, keepdims=True)
        weights = jnp.exp(scores - top)
        total = jnp.sum(weights, axis=-1, keepdims=True)
        weights = (weights / total).astype(jnp.bfloat16)
        mixed = jnp.dot(weights, values, preferred_element_type=jnp.float32)
        attended[:, h * HD : (h + 1) * HD] = mixed.astype(jnp.bfloat16)
    dense[...] = jnp.dot(
        attended[...], dense_w[...], preferred_element_type=jnp.float32
    ).astype(jnp.bfloat16)


def attend(joined, pool, pages, lens, slopes, order, dense_weight, slot):
    count = order.shape[0]
    n_pages = pages.shape[1]
    width = joined.shape[1]
    local_heads = width // (3 * HD)
    page_specs = [
        pl.BlockSpec(
            (1, pool.shape[1], pool.shape[2]),
            functools.partial(lambda p, i, o, pg, ln, sl: (pg[o[i], p], 0, 0), p),
        )
        for p in range(n_pages)
    ]
    return pl.pallas_call(
        functools.partial(attend_body, local_heads, n_pages),
        grid_spec=pltpu.PrefetchScalarGridSpec(
            num_scalar_prefetch=4,
            grid=(count,),
            in_specs=[pl.BlockSpec((slot, width), lambda i, o, pg, ln, sl: (o[i], 0))]
            + page_specs
            + [pl.BlockSpec(dense_weight.shape, lambda i, o, pg, ln, sl: (0, 0))],
            out_specs=[
                pl.BlockSpec((slot, local_heads * HD), lambda i, o, pg, ln, sl: (i, 0)),
                pl.BlockSpec((1, slot, local_heads * 2 * HD), lambda i, o, pg, ln, sl: (i, 0, 0)),
                pl.BlockSpec((slot, dense_weight.shape[1]), lambda i, o, pg, ln, sl: (i, 0)),
            ],
        ),
        out_shape=[
            jax.ShapeDtypeStruct((count * slot, local_heads * HD), jnp.bfloat16),
            jax.ShapeDtypeStruct((count, slot, local_heads * 2 * HD), jnp.bfloat16),
            jax.ShapeDtypeStruct((count * slot, dense_weight.shape[1]), jnp.bfloat16),
        ],
        compiler_params=pltpu.CompilerParams(vmem_limit_bytes=40 * 1024 * 1024),
        cost_estimate=pl.CostEstimate(
            flops=6 * 10**9 * count // 8, bytes_accessed=2 * 10**7 * count // 8, transcendentals=0
        ),
    )(order, pages, lens, slopes, joined, *([pool] * n_pages), dense_weight)


def merge_body(came, fresh, arrived, out):
    here = came[pl.program_id(0)]

    @pl.when(here == 0)
    def _():
        out[...] = fresh[...]

    @pl.when(here != 0)
    def _():
        out[...] = arrived[...]


def merge(fresh, place, arrived, owner, came):
    requests = came.shape[0]
    block = (1,) + fresh.shape[1:]
    return pl.pallas_call(
        lambda place, owner, came, *refs: merge_body(came, *refs),
        grid_spec=pltpu.PrefetchScalarGridSpec(
            num_scalar_prefetch=3,
            grid=(requests,),
            in_specs=[
                pl.BlockSpec(block, lambda i, p, o, c: (p[i], 0, 0)),
                pl.BlockSpec(block, lambda i, p, o, c: (o[i], 0, 0)),
            ],
            out_specs=pl.BlockSpec(block, lambda i, p, o, c: (i, 0, 0)),
        ),
        out_shape=jax.ShapeDtypeStruct(fresh.shape, fresh.dtype),
    )(place, owner, came, fresh, arrived)


def shards(
    tokens,
    first_gain,
    joined_weight,
    dense_weight,
    adapter_down,
    adapter_up,
    adapter_ids,
    adapter_rows,
    second_gain,
    up_weight,
    down_weight,
    page_pool,
    page_table,
    group_index,
    lengths,
    migrants,
    landing,
):
    mlp_count = lax.axis_size("mlp")
    req_count = lax.axis_size("req")
    req_index = lax.axis_index("req")
    mlp_index = lax.axis_index("mlp")
    requests = lengths.shape[0]
    slot = tokens.shape[0] // requests
    width = tokens.shape[1]
    local_heads = joined_weight.shape[1] // (3 * HD)
    own_requests = requests // mlp_count
    rows = mlp_count // CORES
    row_index = mlp_index // CORES
    core_index = mlp_index % CORES
    core_pairs = [(m, m ^ 1) for m in range(mlp_count)]

    def across_rows(values):
        out = [values]
        for k in range(1, rows):
            pairs = [(m, (m + k * CORES) % mlp_count) for m in range(mlp_count)]
            out.append(lax.ppermute(values, "mlp", pairs))
        return out

    local_ids = lax.dynamic_slice_in_dim(adapter_ids, req_index * requests, requests)
    table_rows = adapter_rows[local_ids]
    cols = adapter_down.shape[2]
    own_up = lax.dynamic_slice_in_dim(adapter_up, mlp_index * cols, cols, axis=2)
    own_table = jnp.concatenate([adapter_down, own_up], axis=2)
    own_table, tokens = lax.optimization_barrier((own_table, tokens))
    tables = lax.all_gather(own_table, "req", axis=0, tiled=True)

    normed = layer_norm(tokens, first_gain)
    joined = jnp.dot(normed, joined_weight, preferred_element_type=jnp.float32).astype(jnp.bfloat16)
    pages = page_table[group_index]
    head_pos = (mlp_index * local_heads + jnp.arange(local_heads, dtype=jnp.int32)).astype(
        jnp.float32
    )
    slopes = jnp.exp2(-8.0 * (head_pos + 1.0) / HEADS)

    grid_rows = jnp.arange(rows, dtype=jnp.int32)[None, :]
    grid_cores = (jnp.arange(CORES, dtype=jnp.int32)[:, None] + core_index) % CORES
    orders = [
        ((grid_rows * CORES + grid_cores) * own_requests + c).reshape(-1)
        for c in range(own_requests)
    ]
    half = rows * slot
    firsts = []
    freshes = []
    for c in range(own_requests):
        attended, fresh_c, dense_part = attend(
            joined, page_pool, pages, lengths, slopes, orders[c], dense_weight, slot
        )
        freshes.append(fresh_c)
        firsts.append((attended, dense_part))
    fresh = jnp.concatenate(freshes, axis=0)
    order = jnp.concatenate(orders)
    place = jnp.argmax(
        (order[None, :] == jnp.arange(requests, dtype=jnp.int32)[:, None]).astype(jnp.int32), axis=1
    ).astype(jnp.int32)

    moves = migrants.shape[0]
    my_landing = lax.dynamic_slice_in_dim(landing, req_index * moves, moves)
    own_slots = req_index * requests + jnp.arange(requests, dtype=jnp.int32)
    lands_here = landing[None, :] == own_slots[:, None]
    came = jnp.any(lands_here, axis=1).astype(jnp.int32)
    owner = jnp.argmax(lands_here.astype(jnp.int32), axis=1).astype(jnp.int32) // moves
    hit = my_landing[None, :] // requests == jnp.arange(req_count, dtype=jnp.int32)[:, None]
    leaving = place[jnp.sum(hit.astype(jnp.int32) * migrants[None, :], axis=1)]
    arrived = lax.all_to_all(fresh[leaving], "req", 0, 0, tiled=True)
    owner = jnp.where(came > 0, owner, 0).astype(jnp.int32)

    crossed = []
    for c in range(own_requests):
        dense_part = firsts[c][1]
        other = lax.ppermute(dense_part[half:], "mlp", core_pairs)
        pair_sum = (dense_part[:half].astype(jnp.float32) + other.astype(jnp.float32)).astype(
            jnp.bfloat16
        )
        crossed.append(across_rows(pair_sum))
    barred = lax.optimization_barrier((tables, crossed[0][-1], crossed[-1][0]))
    tables = barred[0]
    chosen = tables[table_rows]
    chosen_down = chosen[:, :, :cols]
    up_parts = [chosen[:, :, cols:]]
    for k in range(1, mlp_count):
        pairs = [(m, (m + k) % mlp_count) for m in range(mlp_count)]
        up_parts.append(lax.ppermute(up_parts[0], "mlp", pairs))
    up_parts = jnp.stack(up_parts, axis=0)
    up_parts = up_parts[(mlp_index - jnp.arange(mlp_count, dtype=jnp.int32)) % mlp_count]

    every = jnp.concatenate([f[0].reshape(mlp_count, slot, local_heads * HD) for f in firsts])
    low_part = lax.dot_general(
        chosen_down[order], every, (((2,), (2,)), ((0,), (0,))), preferred_element_type=jnp.float32
    ).astype(jnp.bfloat16)[place]
    low_all = low_part.astype(jnp.float32)
    for k in range(1, mlp_count):
        pairs = [(m, (m + k) % mlp_count) for m in range(mlp_count)]
        low_all = low_all + lax.ppermute(low_part, "mlp", pairs).astype(jnp.float32)
    low_all = low_all.astype(jnp.bfloat16)

    outs = []
    for c in range(own_requests):
        mine = orders[c][:rows]
        low = low_all.reshape(rows, CORES, own_requests, low_all.shape[1], slot)[:, :, c]
        low = lax.dynamic_index_in_dim(low, core_index, axis=1, keepdims=False)
        own_ups = up_parts[:, mine]
        delta = jnp.concatenate(
            [
                lax.dot_general(
                    low,
                    own_ups[m],
                    (((1,), (1,)), ((0,), (0,))),
                    preferred_element_type=jnp.float32,
                )
                for m in range(mlp_count)
            ],
            axis=2,
        ).reshape(half, width)
        dense = sum(part.astype(jnp.float32) for part in crossed[c])
        own_tokens = tokens.reshape(rows, CORES, own_requests, slot, width)[:, :, c]
        own_tokens = lax.dynamic_index_in_dim(own_tokens, core_index, axis=1, keepdims=False)
        residual = (
            own_tokens.reshape(half, width).astype(jnp.float32) + dense + delta
        ).astype(jnp.bfloat16)
        normed_two = layer_norm(residual, second_gain)
        theirs = lax.ppermute(normed_two, "mlp", core_pairs)
        expanded = gelu_tanh(
            jnp.dot(
                jnp.concatenate([normed_two, theirs], axis=0),
                up_weight,
                preferred_element_type=jnp.float32,
            )
        ).astype(jnp.bfloat16)
        part = jnp.dot(expanded, down_weight, preferred_element_type=jnp.float32).astype(
            jnp.bfloat16
        )
        other = lax.ppermute(part[half:], "mlp", core_pairs)
        pair_sum = (part[:half].astype(jnp.float32) + other.astype(jnp.float32)).astype(
            jnp.bfloat16
        ).reshape(rows, slot, width)
        feed = lax.dynamic_index_in_dim(pair_sum, row_index, axis=0, keepdims=False).astype(
            jnp.float32
        )
        for k in range(1, rows):
            pairs = [(m, (m + k * CORES) % mlp_count) for m in range(mlp_count)]
            send = lax.dynamic_index_in_dim(
                pair_sum, (row_index + k) % rows, axis=0, keepdims=False
            )
            feed = feed + lax.ppermute(send, "mlp", pairs).astype(jnp.float32)
        own_res = lax.dynamic_index_in_dim(
            residual.reshape(rows, slot, width), row_index, axis=0, keepdims=False
        )
        length = lengths[mlp_index * own_requests + c]
        own_valid = jnp.arange(slot, dtype=jnp.int32) < length
        outs.append(
            jnp.where(
                own_valid[:, None], own_res.astype(jnp.float32) + feed, jnp.zeros((), jnp.float32)
            ).astype(jnp.bfloat16)
        )
    layer_out = jnp.concatenate(outs, axis=0)

    page_out = merge(fresh, place, arrived, owner, came)
    return (layer_out, page_out)


def solution(mesh):
    return jax.shard_map(
        shards,
        mesh=mesh,
        in_specs=(
            P("req", None),
            P(),
            P(None, "mlp"),
            P("mlp", None),
            P("req", None, "mlp"),
            P("req", None, None),
            P(),
            P(),
            P(),
            P(None, "mlp"),
            P("mlp", None),
            P("req", None, "mlp"),
            P("req", None),
            P("req"),
            P("req"),
            P("req"),
            P(),
        ),
        out_specs=(P(("req", "mlp"), None), P("req", None, "mlp")),
        check_vma=False,
    )
```

```python
import functools
import math

import jax
import jax.numpy as jnp
from jax import lax
from jax.experimental import pallas as pl
from jax.experimental.pallas import tpu as pltpu
from jax.sharding import PartitionSpec as P

HEADS = 16
HD = 128
ADAPTERS = 64
CORES = 2


EPS = 1e-05


def layer_norm(values, gain):
    values = values.astype(jnp.float32)
    mean = jnp.mean(values, axis=-1, keepdims=True)
    centred = values - mean
    variance = jnp.mean(centred * centred, axis=-1, keepdims=True)
    return (centred * lax.rsqrt(variance + EPS) * gain).astype(jnp.bfloat16)


def gelu_tanh(value):
    return 0.5 * value * (1.0 + jnp.tanh(0.7978845608 * (value + 0.044715 * value * value * value)))


def attend_body(local_heads, n_pages, order, pages, lens, slopes, joined, *refs):
    page_refs = refs[:n_pages]
    dense_w = refs[n_pages]
    attended, fresh, dense = refs[n_pages + 1 :]
    request = order[pl.program_id(0)]
    length = lens[request]
    slot = joined.shape[0]
    pre_len = n_pages * page_refs[0].shape[1]
    total_len = pre_len + slot
    scale = 1.0 / math.sqrt(HD)
    row = lax.broadcasted_iota(jnp.int32, (slot, total_len), 0)
    col = lax.broadcasted_iota(jnp.int32, (slot, total_len), 1)
    distance = (pre_len + row - col).astype(jnp.float32)
    allowed = (col < pre_len) | ((col - pre_len <= row) & (col - pre_len < length))
    valid = lax.broadcasted_iota(jnp.int32, (slot, 2 * HD), 0) < length
    for h in range(local_heads):
        base = h * 3 * HD
        query = joined[:, base : base + HD]
        own = joined[:, base + HD : base + 3 * HD]
        fresh[0, :, h * 2 * HD : (h + 1) * 2 * HD] = jnp.where(
            valid, own, jnp.zeros((), jnp.bfloat16)
        )
        keys = jnp.concatenate(
            [p[0, :, h * 2 * HD : h * 2 * HD + HD] for p in page_refs] + [own[:, :HD]], axis=0
        )
        values = jnp.concatenate(
            [p[0, :, h * 2 * HD + HD : (h + 1) * 2 * HD] for p in page_refs] + [own[:, HD:]],
            axis=0,
        )
        scores = lax.dot_general(
            query, keys, (((1,), (1,)), ((), ())), preferred_element_type=jnp.float32
        )
        scores = jnp.where(allowed, scores * scale - slopes[h] * distance, -jnp.inf)
        top = jnp.max(scores, axis=-1, keepdims=True)
        weights = jnp.exp(scores - top)
        total = jnp.sum(weights, axis=-1, keepdims=True)
        weights = (weights / total).astype(jnp.bfloat16)
        mixed = jnp.dot(weights, values, preferred_element_type=jnp.float32)
        attended[:, h * HD : (h + 1) * HD] = mixed.astype(jnp.bfloat16)
    dense[...] = jnp.dot(
        attended[...], dense_w[...], preferred_element_type=jnp.float32
    ).astype(jnp.bfloat16)


def attend(joined, pool, pages, lens, slopes, order, dense_weight, slot):
    count = order.shape[0]
    n_pages = pages.shape[1]
    width = joined.shape[1]
    local_heads = width // (3 * HD)
    page_specs = [
        pl.BlockSpec(
            (1, pool.shape[1], pool.shape[2]),
            functools.partial(lambda p, i, o, pg, ln, sl: (pg[o[i], p], 0, 0), p),
        )
        for p in range(n_pages)
    ]
    return pl.pallas_call(
        functools.partial(attend_body, local_heads, n_pages),
        grid_spec=pltpu.PrefetchScalarGridSpec(
            num_scalar_prefetch=4,
            grid=(count,),
            in_specs=[pl.BlockSpec((slot, width), lambda i, o, pg, ln, sl: (o[i], 0))]
            + page_specs
            + [pl.BlockSpec(dense_weight.shape, lambda i, o, pg, ln, sl: (0, 0))],
            out_specs=[
                pl.BlockSpec((slot, local_heads * HD), lambda i, o, pg, ln, sl: (i, 0)),
                pl.BlockSpec((1, slot, local_heads * 2 * HD), lambda i, o, pg, ln, sl: (i, 0, 0)),
                pl.BlockSpec((slot, dense_weight.shape[1]), lambda i, o, pg, ln, sl: (i, 0)),
            ],
        ),
        out_shape=[
            jax.ShapeDtypeStruct((count * slot, local_heads * HD), jnp.bfloat16),
            jax.ShapeDtypeStruct((count, slot, local_heads * 2 * HD), jnp.bfloat16),
            jax.ShapeDtypeStruct((count * slot, dense_weight.shape[1]), jnp.bfloat16),
        ],
        compiler_params=pltpu.CompilerParams(vmem_limit_bytes=40 * 1024 * 1024),
        cost_estimate=pl.CostEstimate(
            flops=6 * 10**9 * count // 8, bytes_accessed=2 * 10**7 * count // 8, transcendentals=0
        ),
    )(order, pages, lens, slopes, joined, *([pool] * n_pages), dense_weight)


def merge_body(came, fresh, arrived, out):
    here = came[pl.program_id(0)]

    @pl.when(here == 0)
    def _():
        out[...] = fresh[...]

    @pl.when(here != 0)
    def _():
        out[...] = arrived[...]


def merge(fresh, place, arrived, owner, came):
    requests = came.shape[0]
    block = (1,) + fresh.shape[1:]
    return pl.pallas_call(
        lambda place, owner, came, *refs: merge_body(came, *refs),
        grid_spec=pltpu.PrefetchScalarGridSpec(
            num_scalar_prefetch=3,
            grid=(requests,),
            in_specs=[
                pl.BlockSpec(block, lambda i, p, o, c: (p[i], 0, 0)),
                pl.BlockSpec(block, lambda i, p, o, c: (o[i], 0, 0)),
            ],
            out_specs=pl.BlockSpec(block, lambda i, p, o, c: (i, 0, 0)),
        ),
        out_shape=jax.ShapeDtypeStruct(fresh.shape, fresh.dtype),
    )(place, owner, came, fresh, arrived)


def shards(
    tokens,
    first_gain,
    joined_weight,
    dense_weight,
    adapter_down,
    adapter_up,
    adapter_ids,
    adapter_rows,
    second_gain,
    up_weight,
    down_weight,
    page_pool,
    page_table,
    group_index,
    lengths,
    migrants,
    landing,
):
    mlp_count = lax.axis_size("mlp")
    req_count = lax.axis_size("req")
    req_index = lax.axis_index("req")
    mlp_index = lax.axis_index("mlp")
    requests = lengths.shape[0]
    slot = tokens.shape[0] // requests
    width = tokens.shape[1]
    local_heads = joined_weight.shape[1] // (3 * HD)
    own_requests = requests // mlp_count
    rows = mlp_count // CORES
    row_index = mlp_index // CORES
    core_index = mlp_index % CORES
    core_pairs = [(m, m ^ 1) for m in range(mlp_count)]

    def across_rows(values):
        out = [values]
        for k in range(1, rows):
            pairs = [(m, (m + k * CORES) % mlp_count) for m in range(mlp_count)]
            out.append(lax.ppermute(values, "mlp", pairs))
        return out

    local_ids = lax.dynamic_slice_in_dim(adapter_ids, req_index * requests, requests)
    table_rows = adapter_rows[local_ids]
    cols = adapter_down.shape[2]
    own_up = lax.dynamic_slice_in_dim(adapter_up, mlp_index * cols, cols, axis=2)
    own_table = jnp.concatenate([adapter_down, own_up], axis=2)
    own_table, tokens = lax.optimization_barrier((own_table, tokens))
    tables = lax.all_gather(own_table, "req", axis=0, tiled=True)

    normed = layer_norm(tokens, first_gain)
    joined = jnp.dot(normed, joined_weight, preferred_element_type=jnp.float32).astype(jnp.bfloat16)
    pages = page_table[group_index]
    head_pos = (mlp_index * local_heads + jnp.arange(local_heads, dtype=jnp.int32)).astype(
        jnp.float32
    )
    slopes = jnp.exp2(-8.0 * (head_pos + 1.0) / HEADS)

    grid_rows = jnp.arange(rows, dtype=jnp.int32)[None, :]
    grid_cores = (jnp.arange(CORES, dtype=jnp.int32)[:, None] + core_index) % CORES
    orders = [
        ((grid_rows * CORES + grid_cores) * own_requests + c).reshape(-1)
        for c in range(own_requests)
    ]
    half = rows * slot
    firsts = []
    freshes = []
    for c in range(own_requests):
        attended, fresh_c, dense_part = attend(
            joined, page_pool, pages, lengths, slopes, orders[c], dense_weight, slot
        )
        freshes.append(fresh_c)
        firsts.append((attended, dense_part))
    fresh = jnp.concatenate(freshes, axis=0)
    order = jnp.concatenate(orders)
    place = jnp.argmax(
        (order[None, :] == jnp.arange(requests, dtype=jnp.int32)[:, None]).astype(jnp.int32), axis=1
    ).astype(jnp.int32)

    moves = migrants.shape[0]
    my_landing = lax.dynamic_slice_in_dim(landing, req_index * moves, moves)
    own_slots = req_index * requests + jnp.arange(requests, dtype=jnp.int32)
    lands_here = landing[None, :] == own_slots[:, None]
    came = jnp.any(lands_here, axis=1).astype(jnp.int32)
    owner = jnp.argmax(lands_here.astype(jnp.int32), axis=1).astype(jnp.int32) // moves
    hit = my_landing[None, :] // requests == jnp.arange(req_count, dtype=jnp.int32)[:, None]
    leaving = place[jnp.sum(hit.astype(jnp.int32) * migrants[None, :], axis=1)]
    sending = fresh[leaving]
    arrived = lax.all_to_all(sending, "req", 0, 0, tiled=True)
    owner = jnp.where(came > 0, owner, 0).astype(jnp.int32)

    crossed = []
    for c in range(own_requests):
        dense_part = firsts[c][1]
        other = lax.ppermute(dense_part[half:], "mlp", core_pairs)
        pair_sum = (dense_part[:half].astype(jnp.float32) + other.astype(jnp.float32)).astype(
            jnp.bfloat16
        )
        crossed.append(across_rows(pair_sum))
    early = lax.optimization_barrier((tables, crossed[0][0]))[0]
    up_parts = [early[table_rows][:, :, cols:]]
    for k in range(1, mlp_count):
        pairs = [(m, (m + k) % mlp_count) for m in range(mlp_count)]
        up_parts.append(lax.ppermute(up_parts[0], "mlp", pairs))
    up_parts = jnp.stack(up_parts, axis=0)
    up_parts = up_parts[(mlp_index - jnp.arange(mlp_count, dtype=jnp.int32)) % mlp_count]
    barred = lax.optimization_barrier(
        (tables, crossed[0][-1], crossed[-1][0], up_parts, sending)
    )
    tables, up_parts = barred[0], barred[3]
    chosen_down = tables[table_rows][:, :, :cols]

    every = jnp.concatenate([f[0].reshape(mlp_count, slot, local_heads * HD) for f in firsts])
    low_part = lax.dot_general(
        chosen_down[order], every, (((2,), (2,)), ((0,), (0,))), preferred_element_type=jnp.float32
    ).astype(jnp.bfloat16)[place]
    low_all = low_part.astype(jnp.float32)
    for k in range(1, mlp_count):
        pairs = [(m, (m + k) % mlp_count) for m in range(mlp_count)]
        low_all = low_all + lax.ppermute(low_part, "mlp", pairs).astype(jnp.float32)
    low_all = low_all.astype(jnp.bfloat16)

    outs = []
    for c in range(own_requests):
        if c > 0:
            crossed[c][-1] = lax.optimization_barrier((crossed[c][-1], part))[0]
        mine = orders[c][:rows]
        low = low_all.reshape(rows, CORES, own_requests, low_all.shape[1], slot)[:, :, c]
        low = lax.dynamic_index_in_dim(low, core_index, axis=1, keepdims=False)
        own_ups = up_parts[:, mine]
        delta = jnp.concatenate(
            [
                lax.dot_general(
                    low,
                    own_ups[m],
                    (((1,), (1,)), ((0,), (0,))),
                    preferred_element_type=jnp.float32,
                )
                for m in range(mlp_count)
            ],
            axis=2,
        ).reshape(half, width)
        dense = sum(part.astype(jnp.float32) for part in crossed[c])
        own_tokens = tokens.reshape(rows, CORES, own_requests, slot, width)[:, :, c]
        own_tokens = lax.dynamic_index_in_dim(own_tokens, core_index, axis=1, keepdims=False)
        residual = (
            own_tokens.reshape(half, width).astype(jnp.float32) + dense + delta
        ).astype(jnp.bfloat16)
        normed_two = layer_norm(residual, second_gain)
        theirs = lax.ppermute(normed_two, "mlp", core_pairs)
        expanded = gelu_tanh(
            jnp.dot(
                jnp.concatenate([normed_two, theirs], axis=0),
                up_weight,
                preferred_element_type=jnp.float32,
            )
        ).astype(jnp.bfloat16)
        part = jnp.dot(expanded, down_weight, preferred_element_type=jnp.float32).astype(
            jnp.bfloat16
        )
        other = lax.ppermute(part[half:], "mlp", core_pairs)
        pair_sum = (part[:half].astype(jnp.float32) + other.astype(jnp.float32)).astype(
            jnp.bfloat16
        ).reshape(rows, slot, width)
        feed = lax.dynamic_index_in_dim(pair_sum, row_index, axis=0, keepdims=False).astype(
            jnp.float32
        )
        for k in range(1, rows):
            pairs = [(m, (m + k * CORES) % mlp_count) for m in range(mlp_count)]
            send = lax.dynamic_index_in_dim(
                pair_sum, (row_index + k) % rows, axis=0, keepdims=False
            )
            feed = feed + lax.ppermute(send, "mlp", pairs).astype(jnp.float32)
        own_res = lax.dynamic_index_in_dim(
            residual.reshape(rows, slot, width), row_index, axis=0, keepdims=False
        )
        length = lengths[mlp_index * own_requests + c]
        own_valid = jnp.arange(slot, dtype=jnp.int32) < length
        outs.append(
            jnp.where(
                own_valid[:, None], own_res.astype(jnp.float32) + feed, jnp.zeros((), jnp.float32)
            ).astype(jnp.bfloat16)
        )
    layer_out = jnp.concatenate(outs, axis=0)

    page_out = merge(fresh, place, arrived, owner, came)
    return (layer_out, page_out)


def solution(mesh):
    return jax.shard_map(
        shards,
        mesh=mesh,
        in_specs=(
            P("req", None),
            P(),
            P(None, "mlp"),
            P("mlp", None),
            P("req", None, "mlp"),
            P("req", None, None),
            P(),
            P(),
            P(),
            P(None, "mlp"),
            P("mlp", None),
            P("req", None, "mlp"),
            P("req", None),
            P("req"),
            P("req"),
            P("req"),
            P(),
        ),
        out_specs=(P(("req", "mlp"), None), P("req", None, "mlp")),
        check_vma=False,
    )
```
